32 devices in a mesh: tile: 8 (over z, core), view: 4 (over y, x).
Axes of the slice: x: 2, y: 2, z: 4, core: 2. Of those that a mesh axis runs over, the one named last changes fastest.
Arguments:
- estimate: float32 [256, 128, 256], P('tile'), may hold values from 0.25 to 4
- views_data: bfloat16 [4, 256, 128, 256], P('view', 'tile'), may hold values from 0.25 to 4
- psf_bank: bfloat16 [8, 3, 33], replicated, as said below
- psf_index: int32 [4], P('view'), may hold values from 0 to 7
- margin_extent: int32 [8, 2], P('tile'), may hold values from 1 to 32, as said below
Outputs:
- refined: float32 [256, 128, 256], P('tile')
The draws below stay inside these ranges and needn't reach their ends.
Inputs may be any that keep to these rules, and one draw needn't show every extreme that they name: `psf_bank`: every kernel tap is positive. `margin_extent`: some tile takes exactly 32 cells on some side.
All inputs are finite; a program needn't handle non-finite values.
Results may differ from the reference program's by a relative error of at most 0.00043.
Values may be sent and summed in bfloat16 or wider, within the bound.
No kernel may reach another device: no remote copies, remote signals or barrier semaphores. Data moves between devices by JAX's collectives and lax.ppermute only.
A program may use at most 128 MiB of HBM per device.

```python
import math
import jax
import jax.numpy as jnp
from jax import lax

CORE = 32
SLAB_Y = 128
SLAB_X = 256
MARGIN = 32
TAPS = 33
KERNELS = 8
ITERS = 2
EXT = 96
TILES = 8
VIEWS = 4
DEPTH = 256


def draw_psf_bank(key, part):
    radius = (TAPS - 1) // 2
    key_width, key_rough = jax.random.split(key)
    widths = radius * jnp.exp(jax.random.uniform(key_width, (KERNELS, 3, 1), jnp.float32, jnp.log(0.15), jnp.log(0.5)))
    offsets = jnp.arange(TAPS, dtype=jnp.float32) - radius
    roughness = jax.random.uniform(key_rough, (KERNELS, 3, TAPS), jnp.float32, 0.8, 1.2)
    profile = jnp.exp(-offsets[None, None, :] ** 2 / (2.0 * widths ** 2)) / (widths * 2.5066283)
    return (profile * roughness).astype(jnp.bfloat16)


def draw_margin_extent(key, part):
    key_values, key_place = jax.random.split(key)
    values = jax.random.randint(key_values, (TILES * 2,), 1, MARGIN + 1)
    picked = jax.random.randint(key_place, (), 0, TILES * 2)
    values = jnp.where(jnp.arange(TILES * 2) == picked, MARGIN, values)
    return values.reshape(TILES, 2).astype(jnp.int32)


def touch_ends(entries, stream_key, low, high):
    dims = entries.shape
    index_at = [jax.random.randint(jax.random.fold_in(stream_key, axis), (), 0, dims[axis]) for axis in range(len(dims))]
    entries = entries.at[tuple(index_at)].set(low)
    longest = dims.index(max(dims))
    index_at[longest] = (index_at[longest] + 1) % dims[longest]
    return entries.at[tuple(index_at)].set(high)


def block_levels(key, dims, shards, low, top_value):
    def one(dim, blocks):
        heights = jax.random.uniform(jax.random.fold_in(jax.random.fold_in(key, 6), dim), (blocks,), jnp.float32, low / len(shards), top_value / len(shards))
        return jnp.repeat(jnp.exp(heights), dims[dim] // blocks).reshape((-1,) + (1,) * (len(dims) - dim - 1))

    loudness = one(*shards[0])
    for cut in shards[1:]:
        loudness = loudness * one(*cut)
    return loudness


def setup_inputs(seed: int = 0) -> dict:
    key_list = jax.random.split(jax.random.key(seed), 6)
    return {
        "estimate": jnp.clip(jnp.exp(math.log(4.0) - 2.7725887 * jax.random.uniform(key_list[0], (DEPTH, SLAB_Y, SLAB_X), jnp.float32) ** block_levels(key_list[0], (DEPTH, SLAB_Y, SLAB_X), ((0, 8),), -0.2, 0.2)), 0.25, 4.0),
        "views_data": jnp.clip(jnp.exp(math.log(4.0) - 2.7725887 * jax.random.uniform(key_list[1], (VIEWS, DEPTH, SLAB_Y, SLAB_X), jnp.float32) ** block_levels(key_list[1], (VIEWS, DEPTH, SLAB_Y, SLAB_X), ((0, 4), (1, 8)), -0.2, 0.2)), 0.25, 4.0).astype(jnp.bfloat16),
        "psf_bank": draw_psf_bank(jax.random.fold_in(key_list[5], 71), 0),
        "psf_index": touch_ends(jax.random.randint(key_list[3], (VIEWS,), 0, KERNELS), jax.random.fold_in(key_list[3], 1), 0, KERNELS - 1).astype(jnp.int32),
        "margin_extent": draw_margin_extent(jax.random.fold_in(key_list[5], 71), 0),
    }


def band_matrix(kernel_taps, order):
    radius = (TAPS - 1) // 2
    offsets = jnp.arange(order, dtype=jnp.int32)[None, :] - jnp.arange(order, dtype=jnp.int32)[:, None] + radius
    chosen = offsets[None, :, :] == jnp.arange(TAPS, dtype=jnp.int32)[:, None, None]
    values = kernel_taps.astype(jnp.float32)[:, None, None]
    return jnp.sum(jnp.where(chosen, values, jnp.float32(0.0)), axis=0).astype(jnp.bfloat16)


def view_term(block, measured, kernel_taps, inside):
    depth_band = band_matrix(kernel_taps[0], EXT).astype(jnp.float32)
    row_band = band_matrix(kernel_taps[1], SLAB_Y).astype(jnp.float32)
    col_band = band_matrix(kernel_taps[2], SLAB_X).astype(jnp.float32)
    pass_z = jnp.einsum('ij,jyx->iyx', depth_band, block.astype(jnp.float32)).astype(jnp.bfloat16)
    pass_y = jnp.einsum('ij,zjx->zix', row_band, pass_z.astype(jnp.float32)).astype(jnp.bfloat16)
    blurred = jnp.einsum('zyj,ij->zyi', pass_y.astype(jnp.float32), col_band)
    inside_cells = inside[:, None, None]
    denominator = jnp.where(inside_cells, blurred, jnp.float32(1.0))
    ratio_field = jnp.where(inside_cells, measured.astype(jnp.float32) / denominator, jnp.float32(0.0)).astype(jnp.bfloat16)
    back_x = jnp.einsum('zyi,ij->zyj', ratio_field.astype(jnp.float32), col_band).astype(jnp.bfloat16)
    back_y = jnp.einsum('ij,zix->zjx', row_band, back_x.astype(jnp.float32)).astype(jnp.bfloat16)
    core_band = depth_band[:, MARGIN:MARGIN + CORE]
    return jnp.einsum('ic,iyx->cyx', core_band, back_y.astype(jnp.float32))


def reference(estimate, views_data, psf_bank, psf_index, margin_extent):
    chosen = (jnp.arange(KERNELS, dtype=jnp.int32)[None, :] == psf_index[:, None]).astype(jnp.float32)
    view_taps = jnp.einsum('vk,kat->vat', chosen, psf_bank.astype(jnp.float32)).astype(jnp.bfloat16)
    data_pad = jnp.pad(views_data, ((0, 0), (MARGIN, MARGIN), (0, 0), (0, 0)))
    position = jnp.arange(EXT, dtype=jnp.int32)
    for sweep in range(ITERS):
        est_pad = jnp.pad(estimate.astype(jnp.bfloat16), ((MARGIN, MARGIN), (0, 0), (0, 0)))

        def tile_step(tile_id):
            offset = (tile_id * CORE).astype(jnp.int32)
            global_pos = offset - MARGIN + position
            lower_ext = margin_extent[tile_id, 0]
            upper_ext = margin_extent[tile_id, 1]
            inside = (position >= MARGIN - lower_ext) & (position < MARGIN + CORE + upper_ext)
            inside = inside & (global_pos >= 0) & (global_pos < DEPTH)
            block = lax.dynamic_slice_in_dim(est_pad, offset, EXT, 0)
            block = jnp.where(inside[:, None, None], block, jnp.zeros_like(block))

            def view_step(summed, view_id):
                measured = lax.dynamic_slice_in_dim(data_pad[view_id], offset, EXT, 0)
                return summed + view_term(block, measured, view_taps[view_id], inside), None

            summed, unused = lax.scan(view_step, jnp.zeros((CORE, SLAB_Y, SLAB_X), jnp.float32), jnp.arange(VIEWS, dtype=jnp.int32))
            current = lax.dynamic_slice_in_dim(estimate, offset, CORE, 0)
            return current * summed / VIEWS

        estimate = lax.map(tile_step, jnp.arange(TILES, dtype=jnp.int32)).reshape(DEPTH, SLAB_Y, SLAB_X)
    return estimate
```

```python
import functools

import jax
import jax.numpy as jnp
from jax import lax
from jax.experimental import pallas as pl
from jax.experimental.pallas import tpu as pltpu
from jax.sharding import PartitionSpec as P

MARGIN = 32
ITERS = 2
REACH = 16
LEVELS = 32766.0
LANES = 128
GROUP = 4


def dot32(a, b):
    return jnp.dot(a, b, preferred_element_type=jnp.float32)


def halves(value):
    return [value[:, h * LANES : (h + 1) * LANES] for h in range(value.shape[1] // LANES)]


def sweep_kernel(plan, *refs):
    pieces_in, pieces_out, depths, core, rows, cols = plan
    refs = list(refs)
    take = lambda n: [refs.pop(0) for _ in range(n)]
    (mask_ref,) = take(1)
    lows, owns, highs = take(pieces_in), take(pieces_in), take(pieces_in)
    meas_low, meas_own, meas_high = take(3)
    z_band, z_back, y_band, y_back, x_band, x_back = take(6)
    codes, scales = take(pieces_out), take(pieces_out)
    by_plane, by_row = take(2)
    lane_parts = cols // LANES

    rows_in = rows // pieces_in
    for p in range(pieces_in):

        def z_pass(step, carry, p=p):
            for u in range(2):
                y = step * 2 + u
                block = jnp.concatenate([lows[p][y], owns[p][y], highs[p][y]], axis=0)
                out = dot32(z_band[...], block)
                for h, part in enumerate(halves(out)):
                    by_plane[h, pl.ds(p * rows_in + y, depths, stride=rows), :] = part
            return carry

        lax.fori_loop(0, rows_in // 2, z_pass, 0)

    def planes(first, measured, count):
        def body(step, carry):
            passed = []
            for g in range(GROUP):
                k = first + step * GROUP + g
                start = pl.multiple_of(k * rows, rows)
                plane = jnp.concatenate(
                    [by_plane[h, pl.ds(start, rows), :].astype(jnp.bfloat16) for h in range(lane_parts)],
                    axis=1,
                )
                passed.append(dot32(y_band[...], plane).astype(jnp.bfloat16))
            blurred = dot32(jnp.concatenate(passed, axis=0), x_band[...])
            ratios = []
            for g in range(GROUP):
                k = first + step * GROUP + g
                inside = mask_ref[k] > 0
                data = measured[step * GROUP + g].astype(jnp.float32)
                under = jnp.where(inside, blurred[g * rows : (g + 1) * rows], jnp.float32(1.0))
                ratios.append(jnp.where(inside, data / under, jnp.float32(0.0)).astype(jnp.bfloat16))
            back = dot32(jnp.concatenate(ratios, axis=0), x_back[...]).astype(jnp.bfloat16)
            for g in range(GROUP):
                k = first + step * GROUP + g
                out = dot32(y_back[...], back[g * rows : (g + 1) * rows])
                for h, part in enumerate(halves(out)):
                    by_row[h, pl.ds(k, rows, stride=depths), :] = part
            return carry

        lax.fori_loop(0, count // GROUP, body, 0)

    planes(0, meas_low, REACH)
    planes(REACH, meas_own, core)
    planes(REACH + core, meas_high, REACH)

    rows_out = rows // pieces_out
    for p in range(pieces_out):

        def z_return(step, carry, p=p):
            for u in range(2):
                y = step * 2 + u
                start = pl.multiple_of((p * rows_out + y) * depths, depths)
                column = jnp.concatenate(
                    [by_row[h, pl.ds(start, depths), :].astype(jnp.bfloat16) for h in range(lane_parts)],
                    axis=1,
                )
                term = dot32(z_back[...], column)
                top = jnp.maximum(jnp.max(jnp.abs(term), axis=0, keepdims=True), jnp.float32(1e-30))
                codes[p][y] = jnp.round(term * (LEVELS / top)).astype(jnp.int32).astype(jnp.int16)
                scales[p][pl.ds(y, 1), :] = top * jnp.float32(1.0 / LEVELS)
            return carry

        lax.fori_loop(0, rows_out // 2, z_return, 0)


def sweep(mask, lows, owns, highs, measured, bands, pieces_out):
    core, (rows, cols) = measured[1].shape[0], measured[1].shape[1:]
    depths = core + 2 * REACH
    plan = (len(owns), pieces_out, depths, core, rows, cols)
    rows_out = rows // pieces_out
    vmem = pl.BlockSpec(memory_space=pltpu.VMEM)
    out = pl.pallas_call(
        functools.partial(sweep_kernel, plan),
        out_shape=[jax.ShapeDtypeStruct((rows_out, core, cols), jnp.int16)] * pieces_out
        + [jax.ShapeDtypeStruct((rows_out, cols), jnp.float32)] * pieces_out,
        in_specs=[pl.BlockSpec(memory_space=pltpu.SMEM)] + [vmem] * (3 * len(owns) + 9),
        out_specs=[vmem] * (2 * pieces_out),
        scratch_shapes=[
            pltpu.VMEM((cols // LANES, depths * rows, LANES), jnp.float32),
            pltpu.VMEM((cols // LANES, rows * depths, LANES), jnp.float32),
        ],
        compiler_params=pltpu.CompilerParams(vmem_limit_bytes=56 * 1024 * 1024),
        name="sweep",
    )(mask, *lows, *owns, *highs, *measured, *bands)
    return out[:pieces_out], out[pieces_out:]


def band(taps, row_index, col_index):
    count = taps.shape[0]
    offsets = col_index[None, :] - row_index[:, None] + (count - 1) // 2
    chosen = offsets[None, :, :] == jnp.arange(count, dtype=jnp.int32)[:, None, None]
    return jnp.sum(jnp.where(chosen, taps[:, None, None], jnp.float32(0.0)), axis=0)


def encode(values, axis):
    top = jnp.maximum(jnp.max(jnp.abs(values), axis=axis, keepdims=True), jnp.float32(1e-30))
    code = jnp.round(values * (LEVELS / top)).astype(jnp.int32).astype(jnp.int16)
    return code, top * jnp.float32(1.0 / LEVELS)


def on_device(estimate, views_data, psf_bank, psf_index, margin_extent):
    core, rows, cols = estimate.shape
    kernels_count = psf_bank.shape[0]
    tiles = lax.axis_size("tile")
    views = lax.axis_size("view")
    tile_id = lax.axis_index("tile")
    view_id = lax.axis_index("view")
    rows_piece = rows // views
    forward = [(i, i + 1) for i in range(tiles - 1)]
    backward = [(target, source) for source, target in forward]

    def from_below(x):
        return lax.ppermute(x, "tile", forward)

    def from_above(x):
        return lax.ppermute(x, "tile", backward)

    def from_view(x, bits):
        return lax.ppermute(x, "view", [(v, v ^ bits) for v in range(views)])

    start = jnp.transpose(estimate.astype(jnp.bfloat16), (1, 0, 2))
    low, high = from_below(start), from_above(start)
    data = views_data[0]
    measured = (
        from_below(data[core - REACH :]),
        data,
        from_above(data[:REACH]),
    )

    chosen = (jnp.arange(kernels_count, dtype=jnp.int32) == psf_index[0]).astype(jnp.float32)
    taps = jnp.einsum("k,kat->at", chosen, psf_bank.astype(jnp.float32))
    position = jnp.arange(core + 2 * MARGIN, dtype=jnp.int32)
    global_pos = tile_id * core - MARGIN + position
    inside = (position >= MARGIN - margin_extent[0, 0]) & (
        position < MARGIN + core + margin_extent[0, 1]
    )
    inside = inside & (global_pos >= 0) & (global_pos < core * tiles)
    wanted = jnp.arange(core + 2 * REACH, dtype=jnp.int32) + (MARGIN - REACH)
    cores = jnp.arange(core, dtype=jnp.int32) + MARGIN
    natural = jnp.arange(rows, dtype=jnp.int32)
    held = ((natural // rows_piece) ^ view_id) * rows_piece + natural % rows_piece
    columns = jnp.arange(cols, dtype=jnp.int32)
    half = jnp.bfloat16
    z_band = jnp.where(inside[None, :], band(taps[0], wanted, position), 0.0).astype(half)
    z_back = band(taps[0], wanted, cores).T.astype(half)
    y_natural = band(taps[1], natural, natural).astype(half)
    y_held = band(taps[1], natural, held).astype(half)
    y_back = y_held.T
    x_back = band(taps[2], columns, columns).astype(half)
    x_band = x_back.T
    mask = lax.slice_in_dim(inside, MARGIN - REACH, MARGIN + core + REACH).astype(jnp.int32)

    mine = jnp.transpose(
        lax.dynamic_slice_in_dim(estimate, view_id * rows_piece, rows_piece, axis=1), (1, 0, 2)
    )
    lows, owns, highs = [low], [start], [high]
    for it in range(ITERS):
        bands = (z_band, z_back, y_natural if it == 0 else y_held, y_back, x_band, x_back)
        codes, scales = sweep(mask, lows, owns, highs, measured, bands, views)
        total = codes[0].astype(jnp.float32) * scales[0][:, None, :]
        for bits in range(1, views):
            code, scale = from_view(codes[bits], bits), from_view(scales[bits], bits)
            total = total + code.astype(jnp.float32) * scale[:, None, :]
        mine = mine * total / views
        if it + 1 < ITERS:
            rounded = mine.astype(half)
            owns = [rounded] + [from_view(rounded, bits) for bits in range(1, views)]
            lows = [from_below(x) for x in owns]
            highs = [from_above(x) for x in owns]
    code, scale = encode(jnp.transpose(mine, (1, 0, 2)), 0)
    out = jnp.zeros((core, rows, cols), jnp.float32)
    for bits in range(views):
        c, s = (code, scale) if bits == 0 else (from_view(code, bits), from_view(scale, bits))
        piece = c.astype(jnp.float32) * s
        out = lax.dynamic_update_slice_in_dim(out, piece, (view_id ^ bits) * rows_piece, axis=1)
    return out


def solution(mesh):
    return jax.shard_map(
        on_device,
        mesh=mesh,
        in_specs=(
            P("tile", None, None),
            P("view", "tile", None, None),
            P(),
            P("view"),
            P("tile", None),
        ),
        out_specs=P("tile", None, None),
        check_vma=False,
    )
```

```python
import functools

import jax
import jax.numpy as jnp
from jax import lax
from jax.experimental import pallas as pl
from jax.experimental.pallas import tpu as pltpu
from jax.sharding import PartitionSpec as P

MARGIN = 32
ITERS = 2
REACH = 16
LEVELS = 32766.0
LANES = 128
GROUP = 16
UNROLL = 32
PAD = 8


def dot32(a, b):
    return jnp.dot(a, b, preferred_element_type=jnp.float32)


def halves(value):
    return [value[:, h * LANES : (h + 1) * LANES] for h in range(value.shape[1] // LANES)]


def sweep_kernel(plan, *refs):
    pieces_in, pieces_out, depths, core, rows, cols = plan
    refs = list(refs)
    take = lambda n: [refs.pop(0) for _ in range(n)]
    (mask_ref,) = take(1)
    lows, owns, highs = take(pieces_in), take(pieces_in), take(pieces_in)
    meas_low, meas_own, meas_high = take(3)
    z_band, z_back, y_band, y_back, x_band, x_back = take(6)
    codes, scales = take(pieces_out), take(pieces_out)
    by_plane, by_row = take(2)
    lane_parts = cols // LANES
    plane_rows, row_depths = rows + PAD, depths + PAD

    rows_in = rows // pieces_in
    unroll_in = min(UNROLL, rows_in)
    for p in range(pieces_in):

        def z_pass(step, carry, p=p):
            for u in range(unroll_in):
                y = step * unroll_in + u
                block = jnp.concatenate([lows[p][y], owns[p][y], highs[p][y]], axis=0)
                out = dot32(z_band[...], block)
                for h, part in enumerate(halves(out)):
                    by_plane[h, pl.ds(p * rows_in + y, depths, stride=plane_rows), :] = part
            return carry

        lax.fori_loop(0, rows_in // unroll_in, z_pass, 0)

    def planes(first, measured, count):
        def body(step, carry):
            passed = []
            for g in range(GROUP):
                k = first + step * GROUP + g
                start = pl.multiple_of(k * plane_rows, PAD)
                plane = jnp.concatenate(
                    [by_plane[h, pl.ds(start, rows), :].astype(jnp.bfloat16) for h in range(lane_parts)],
                    axis=1,
                )
                passed.append(dot32(y_band[...], plane).astype(jnp.bfloat16))
            blurred = dot32(jnp.concatenate(passed, axis=0), x_band[...])
            ratios = []
            for g in range(GROUP):
                k = first + step * GROUP + g
                inside = mask_ref[k] > 0
                data = measured[step * GROUP + g].astype(jnp.float32)
                under = jnp.where(inside, blurred[g * rows : (g + 1) * rows], jnp.float32(1.0))
                ratios.append(jnp.where(inside, data / under, jnp.float32(0.0)).astype(jnp.bfloat16))
            back = dot32(jnp.concatenate(ratios, axis=0), x_back[...]).astype(jnp.bfloat16)
            for g in range(GROUP):
                k = first + step * GROUP + g
                out = dot32(y_back[...], back[g * rows : (g + 1) * rows])
                for h, part in enumerate(halves(out)):
                    by_row[h, pl.ds(k, rows, stride=row_depths), :] = part
            return carry

        lax.fori_loop(0, count // GROUP, body, 0)

    planes(0, meas_low, REACH)
    planes(REACH, meas_own, core)
    planes(REACH + core, meas_high, REACH)

    rows_out = rows // pieces_out
    unroll_out = min(UNROLL, rows_out)
    for p in range(pieces_out):

        def z_return(step, carry, p=p):
            for u in range(unroll_out):
                y = step * unroll_out + u
                start = pl.multiple_of((p * rows_out + y) * row_depths, PAD)
                column = jnp.concatenate(
                    [by_row[h, pl.ds(start, depths), :].astype(jnp.bfloat16) for h in range(lane_parts)],
                    axis=1,
                )
                term = dot32(z_back[...], column)
                top = jnp.maximum(jnp.max(jnp.abs(term), axis=0, keepdims=True), jnp.float32(1e-30))
                codes[p][y] = jnp.round(term * (LEVELS / top)).astype(jnp.int32).astype(jnp.int16)
                scales[p][pl.ds(y, 1), :] = top * jnp.float32(1.0 / LEVELS)
            return carry

        lax.fori_loop(0, rows_out // unroll_out, z_return, 0)


def sweep(mask, lows, owns, highs, measured, bands, pieces_out):
    core, (rows, cols) = measured[1].shape[0], measured[1].shape[1:]
    depths = core + 2 * REACH
    plan = (len(owns), pieces_out, depths, core, rows, cols)
    rows_out = rows // pieces_out
    vmem = pl.BlockSpec(memory_space=pltpu.VMEM)
    out = pl.pallas_call(
        functools.partial(sweep_kernel, plan),
        out_shape=[jax.ShapeDtypeStruct((rows_out, core, cols), jnp.int16)] * pieces_out
        + [jax.ShapeDtypeStruct((rows_out, cols), jnp.float32)] * pieces_out,
        in_specs=[pl.BlockSpec(memory_space=pltpu.SMEM)] + [vmem] * (3 * len(owns) + 9),
        out_specs=[vmem] * (2 * pieces_out),
        scratch_shapes=[
            pltpu.VMEM((cols // LANES, depths * (rows + PAD), LANES), jnp.float32),
            pltpu.VMEM((cols // LANES, rows * (depths + PAD), LANES), jnp.float32),
        ],
        compiler_params=pltpu.CompilerParams(vmem_limit_bytes=56 * 1024 * 1024),
        name="sweep",
    )(mask, *lows, *owns, *highs, *measured, *bands)
    return out[:pieces_out], out[pieces_out:]


def band(taps, row_index, col_index):
    count = taps.shape[0]
    offsets = col_index[None, :] - row_index[:, None] + (count - 1) // 2
    chosen = offsets[None, :, :] == jnp.arange(count, dtype=jnp.int32)[:, None, None]
    return jnp.sum(jnp.where(chosen, taps[:, None, None], jnp.float32(0.0)), axis=0)


def encode(values, axis):
    top = jnp.maximum(jnp.max(jnp.abs(values), axis=axis, keepdims=True), jnp.float32(1e-30))
    code = jnp.round(values * (LEVELS / top)).astype(jnp.int32).astype(jnp.int16)
    return code, top * jnp.float32(1.0 / LEVELS)


def on_device(estimate, views_data, psf_bank, psf_index, margin_extent):
    core, rows, cols = estimate.shape
    kernels_count = psf_bank.shape[0]
    tiles = lax.axis_size("tile")
    views = lax.axis_size("view")
    tile_id = lax.axis_index("tile")
    view_id = lax.axis_index("view")
    rows_piece = rows // views
    forward = [(i, i + 1) for i in range(tiles - 1)]
    backward = [(target, source) for source, target in forward]

    def from_below(x):
        return lax.ppermute(x, "tile", forward)

    def from_above(x):
        return lax.ppermute(x, "tile", backward)

    def from_view(x, bits):
        return lax.ppermute(x, "view", [(v, v ^ bits) for v in range(views)])

    data = views_data[0]
    measured = (
        from_below(data[core - REACH :]),
        data,
        from_above(data[:REACH]),
    )
    start = jnp.transpose(estimate.astype(jnp.bfloat16), (1, 0, 2))
    low, high = from_below(start), from_above(start)

    chosen = (jnp.arange(kernels_count, dtype=jnp.int32) == psf_index[0]).astype(jnp.float32)
    taps = jnp.einsum("k,kat->at", chosen, psf_bank.astype(jnp.float32))
    position = jnp.arange(core + 2 * MARGIN, dtype=jnp.int32)
    global_pos = tile_id * core - MARGIN + position
    inside = (position >= MARGIN - margin_extent[0, 0]) & (
        position < MARGIN + core + margin_extent[0, 1]
    )
    inside = inside & (global_pos >= 0) & (global_pos < core * tiles)
    wanted = jnp.arange(core + 2 * REACH, dtype=jnp.int32) + (MARGIN - REACH)
    cores = jnp.arange(core, dtype=jnp.int32) + MARGIN
    natural = jnp.arange(rows, dtype=jnp.int32)
    held = ((natural // rows_piece) ^ view_id) * rows_piece + natural % rows_piece
    columns = jnp.arange(cols, dtype=jnp.int32)
    half = jnp.bfloat16
    z_band = jnp.where(inside[None, :], band(taps[0], wanted, position), 0.0).astype(half)
    z_back = band(taps[0], wanted, cores).T.astype(half)
    y_natural = band(taps[1], natural, natural).astype(half)
    y_held = band(taps[1], natural, held).astype(half)
    y_back = y_held.T
    x_back = band(taps[2], columns, columns).astype(half)
    x_band = x_back.T
    mask = lax.slice_in_dim(inside, MARGIN - REACH, MARGIN + core + REACH).astype(jnp.int32)

    mine = jnp.transpose(
        lax.dynamic_slice_in_dim(estimate, view_id * rows_piece, rows_piece, axis=1), (1, 0, 2)
    )
    lows, owns, highs = [low], [start], [high]
    for it in range(ITERS):
        bands = (z_band, z_back, y_natural if it == 0 else y_held, y_back, x_band, x_back)
        codes, scales = sweep(mask, lows, owns, highs, measured, bands, views)
        total = codes[0].astype(jnp.float32) * scales[0][:, None, :]
        for bits in range(1, views):
            code, scale = from_view(codes[bits], bits), from_view(scales[bits], bits)
            total = total + code.astype(jnp.float32) * scale[:, None, :]
        mine = mine * total / views
        if it + 1 < ITERS:
            rounded = mine.astype(half)
            owns = [rounded] + [from_view(rounded, bits) for bits in range(1, views)]
            lows = [from_below(x) for x in owns]
            highs = [from_above(x) for x in owns]
    code, scale = encode(jnp.transpose(mine, (1, 0, 2)), 0)
    out = jnp.zeros((core, rows, cols), jnp.float32)
    for bits in range(views):
        c, s = (code, scale) if bits == 0 else (from_view(code, bits), from_view(scale, bits))
        piece = c.astype(jnp.float32) * s
        out = lax.dynamic_update_slice_in_dim(out, piece, (view_id ^ bits) * rows_piece, axis=1)
    return out


def solution(mesh):
    return jax.shard_map(
        on_device,
        mesh=mesh,
        in_specs=(
            P("tile", None, None),
            P("view", "tile", None, None),
            P(),
            P("view"),
            P("tile", None),
        ),
        out_specs=P("tile", None, None),
        check_vma=False,
    )
```

```python
import functools

import jax
import jax.numpy as jnp
from jax import lax
from jax.experimental import pallas as pl
from jax.experimental.pallas import tpu as pltpu
from jax.sharding import PartitionSpec as P

MARGIN = 32
ITERS = 2
REACH = 16
LANES = 128
GROUP = 16
UNROLL = 32
PAD = 8
STEPS = 8.0
ROOM = 32768.0 / 32000.0
SMALL = 1e-30
VMEM_LIMIT = 56 * 1024 * 1024
ANY = pl.BlockSpec(memory_space=pl.ANY)
VMEM = pl.BlockSpec(memory_space=pltpu.VMEM)
SMEM = pl.BlockSpec(memory_space=pltpu.SMEM)


def dot32(a, b):
    return jnp.dot(a, b, preferred_element_type=jnp.float32)


def halves(value):
    return [value[:, h * LANES : (h + 1) * LANES] for h in range(value.shape[1] // LANES)]


def encode(values):
    top = jnp.maximum(jnp.max(jnp.abs(values), axis=0, keepdims=True), jnp.float32(SMALL))
    power = jnp.ceil(jnp.log2(top * jnp.float32(ROOM)) * jnp.float32(STEPS))
    code = jnp.round(values * jnp.exp2(15.0 - power * jnp.float32(1.0 / STEPS)))
    return code.astype(jnp.int32).astype(jnp.int16), power


def scale_of(powers):
    return jnp.exp2(powers.astype(jnp.float32) * jnp.float32(1.0 / STEPS) - 15.0)


def put_powers(slab_ref, powers):
    depth, count = slab_ref.shape[0], powers.shape[0]
    slab_ref[0:count, :] = powers.astype(jnp.int32).astype(jnp.int16)
    if count < depth:
        slab_ref[count:depth, :] = jnp.zeros((depth - count, powers.shape[1]), jnp.int16)


def sweep_kernel(plan, *refs):
    pieces, shares, pieces_out, core, rows, cols = plan
    refs = list(refs)
    take = lambda n: [refs.pop(0) for _ in range(n)]
    view_ref, mask_ref = take(2)
    sources = [take(n) for n in shares]
    data_sources = take(3)
    z_band, z_back, y_band, y_back, x_band, x_back = take(6)
    outs = take(pieces_out)
    block, measured, by_plane, by_row, codes, powers, in_sem, data_sem, out_sem = refs
    depths = core + 2 * REACH
    lane_parts = cols // LANES
    plane_rows, row_depths = rows + PAD, depths + PAD
    rows_out = rows // pieces_out
    unroll_out = min(UNROLL, rows_out)

    def block_copies(index):
        bits, offset, count = pieces[index]
        copies = []
        for part, given in enumerate(sources):
            if len(given) == 1:
                first = (view_ref[0] ^ bits) * rows_out + offset
                source = given[0].at[pl.ds(first, count)]
            else:
                source = given[index]
            target = block.at[pl.ds(bits * rows_out + offset, count), pl.ds(part * core, core)]
            copies.append(pltpu.make_async_copy(source, target, in_sem.at[part, index]))
        return copies

    starts = (0, REACH, REACH + core)
    counts = (REACH, core, REACH)
    data_copies = [
        pltpu.make_async_copy(
            data_sources[i], measured.at[pl.ds(starts[i], counts[i])], data_sem.at[i]
        )
        for i in range(3)
    ]
    for index in range(len(pieces)):
        for copy in block_copies(index):
            copy.start()
    for copy in data_copies:
        copy.start()

    for index, (bits, offset, count) in enumerate(pieces):
        for copy in block_copies(index):
            copy.wait()
        for y in range(bits * rows_out + offset, bits * rows_out + offset + count):
            for h, part in enumerate(halves(dot32(z_band[...], block[y]))):
                by_plane[h, pl.ds(y, depths, stride=plane_rows), :] = part
    for copy in data_copies:
        copy.wait()

    def planes(step, carry):
        passed = []
        for g in range(GROUP):
            start = pl.multiple_of((step * GROUP + g) * plane_rows, PAD)
            plane = jnp.concatenate(
                [by_plane[h, pl.ds(start, rows), :].astype(jnp.bfloat16) for h in range(lane_parts)],
                axis=1,
            )
            passed.append(dot32(y_band[...], plane).astype(jnp.bfloat16))
        blurred = dot32(jnp.concatenate(passed, axis=0), x_band[...])
        ratios = []
        for g in range(GROUP):
            k = step * GROUP + g
            inside = mask_ref[k] > 0
            data = measured[k].astype(jnp.float32)
            under = jnp.where(inside, blurred[g * rows : (g + 1) * rows], jnp.float32(1.0))
            ratios.append(jnp.where(inside, data / under, jnp.float32(0.0)).astype(jnp.bfloat16))
        back = dot32(jnp.concatenate(ratios, axis=0), x_back[...]).astype(jnp.bfloat16)
        for g in range(GROUP):
            out = dot32(y_back[...], back[g * rows : (g + 1) * rows])
            for h, part in enumerate(halves(out)):
                by_row[h, pl.ds(step * GROUP + g, rows, stride=row_depths), :] = part
        return carry

    lax.fori_loop(0, depths // GROUP, planes, 0)

    out_copies = []
    for p in range(pieces_out):

        def z_return(step, carry, p=p):
            for u in range(unroll_out):
                y = step * unroll_out + u
                start = pl.multiple_of((p * rows_out + y) * row_depths, PAD)
                column = jnp.concatenate(
                    [by_row[h, pl.ds(start, depths), :].astype(jnp.bfloat16) for h in range(lane_parts)],
                    axis=1,
                )
                code, power = encode(dot32(z_back[...], column))
                codes[p, y] = code
                powers[pl.ds(y, 1), :] = power
            return carry

        lax.fori_loop(0, rows_out // unroll_out, z_return, 0)
        put_powers(codes.at[p, rows_out], powers[...])
        copy = pltpu.make_async_copy(codes.at[p], outs[p], out_sem.at[p])
        copy.start()
        out_copies.append(copy)
    for copy in out_copies:
        copy.wait()


def sweep(view_id, mask, pieces, blocks, measured, bands, pieces_out):
    core, (rows, cols) = measured[1].shape[0], measured[1].shape[1:]
    depths = core + 2 * REACH
    rows_out = rows // pieces_out
    shares = tuple(len(part) for part in blocks)
    flat = [piece for part in blocks for piece in part]
    return pl.pallas_call(
        functools.partial(sweep_kernel, (pieces, shares, pieces_out, core, rows, cols)),
        out_shape=[jax.ShapeDtypeStruct((rows_out + 1, core, cols), jnp.int16)] * pieces_out,
        in_specs=[SMEM] * 2 + [ANY] * (len(flat) + 3) + [VMEM] * 6,
        out_specs=[ANY] * pieces_out,
        scratch_shapes=[
            pltpu.VMEM((rows, 3 * core, cols), jnp.bfloat16),
            pltpu.VMEM((depths, rows, cols), jnp.bfloat16),
            pltpu.VMEM((cols // LANES, depths * (rows + PAD), LANES), jnp.float32),
            pltpu.VMEM((cols // LANES, rows * (depths + PAD), LANES), jnp.float32),
            pltpu.VMEM((pieces_out, rows_out + 1, core, cols), jnp.int16),
            pltpu.VMEM((rows_out, cols), jnp.float32),
            pltpu.SemaphoreType.DMA((3, len(pieces))),
            pltpu.SemaphoreType.DMA((3,)),
            pltpu.SemaphoreType.DMA((pieces_out,)),
        ],
        compiler_params=pltpu.CompilerParams(vmem_limit_bytes=VMEM_LIMIT),
        name="sweep",
    )(view_id, mask, *flat, *measured, *bands)


def update_kernel(last, views, *refs):
    codes, mine, outs = refs[:views], refs[views], refs[views + 1 :]
    count = mine.shape[0]
    scales = [scale_of(code[count][0:count]) for code in codes]
    powers = []
    for y in range(count):
        total = sum(
            code[y].astype(jnp.float32) * scale[y : y + 1] for code, scale in zip(codes, scales)
        )
        value = mine[y] * total * jnp.float32(1.0 / views)
        if last:
            outs[0][y], power = encode(value)
            powers.append(power)
        else:
            outs[0][y] = value
            outs[1][y] = value.astype(jnp.bfloat16)
    if last:
        put_powers(outs[0].at[count], jnp.concatenate(powers, axis=0))


def update(codes, mine, last):
    views = len(codes)
    if last:
        shapes = [jax.ShapeDtypeStruct(codes[0].shape, jnp.int16)]
    else:
        shapes = [jax.ShapeDtypeStruct(mine.shape, t) for t in (jnp.float32, jnp.bfloat16)]
    return pl.pallas_call(
        functools.partial(update_kernel, last, views),
        out_shape=shapes,
        in_specs=[VMEM] * (views + 1),
        out_specs=[VMEM] * len(shapes),
        compiler_params=pltpu.CompilerParams(vmem_limit_bytes=VMEM_LIMIT),
        name="update",
    )(*codes, mine)


def gather_kernel(pieces, rows_piece, core, rows, cols, *refs):
    n = len(pieces)
    view_ref, codes, out, planes, sem = refs[0], refs[1 : n + 1], *refs[n + 1 :]
    plane_rows = rows + PAD
    for code, (bits, offset, count) in zip(codes, pieces):
        base = (view_ref[0] ^ bits) * rows_piece + offset
        scale = scale_of(code[count][0:rows_piece])
        for y in range(count):
            value = code[y].astype(jnp.float32) * scale[offset + y : offset + y + 1]
            for h, part in enumerate(halves(value)):
                planes[h, pl.ds(base + y, core, stride=plane_rows), :] = part
    copies = [
        pltpu.make_async_copy(
            planes.at[h, pl.ds(z * plane_rows, rows)],
            out.at[z, :, pl.ds(h * LANES, LANES)],
            sem.at[h, z],
        )
        for z in range(core)
        for h in range(cols // LANES)
    ]
    for copy in copies:
        copy.start()
    for copy in copies:
        copy.wait()


def gather(view_id, pieces, codes, rows, views):
    core, cols = codes[0].shape[1:]
    return pl.pallas_call(
        functools.partial(gather_kernel, pieces, rows // views, core, rows, cols),
        out_shape=jax.ShapeDtypeStruct((core, rows, cols), jnp.float32),
        in_specs=[SMEM] + [VMEM] * len(codes),
        out_specs=ANY,
        scratch_shapes=[
            pltpu.VMEM((cols // LANES, core * (rows + PAD), LANES), jnp.float32),
            pltpu.SemaphoreType.DMA((cols // LANES, core)),
        ],
        compiler_params=pltpu.CompilerParams(vmem_limit_bytes=VMEM_LIMIT),
        name="gather",
    )(view_id, *codes)


def band(taps, row_index, col_index):
    count = taps.shape[0]
    offsets = col_index[None, :] - row_index[:, None] + (count - 1) // 2
    chosen = offsets[None, :, :] == jnp.arange(count, dtype=jnp.int32)[:, None, None]
    return jnp.sum(jnp.where(chosen, taps[:, None, None], jnp.float32(0.0)), axis=0)


def on_device(estimate, views_data, psf_bank, psf_index, margin_extent):
    core, rows, cols = estimate.shape
    kernels_count = psf_bank.shape[0]
    tiles = lax.axis_size("tile")
    views = lax.axis_size("view")
    tile_id = lax.axis_index("tile")
    view_id = lax.axis_index("view")
    rows_piece = rows // views
    half = jnp.bfloat16

    near_pairs = [(t, t ^ 1) for t in range(tiles)]
    far_pairs = [(t, ((t + 1) ^ 1) - 1) for t in range(1, tiles - 1)]
    even = tile_id % 2 == 0

    def far(x):
        return lax.ppermute(x, "tile", far_pairs)

    def near(x):
        return lax.ppermute(x, "tile", near_pairs)

    def from_view(x, bits):
        return lax.ppermute(x, "view", [(v, v ^ bits) for v in range(views)])

    part = rows_piece // 2
    if views == 4:
        pieces = ((0, 0, rows_piece), (1, 0, rows_piece), (2, 0, rows_piece), (3, 0, part), (3, part, part))
    else:
        pieces = tuple((bits, 0, rows_piece) for bits in range(views))

    def share(x):
        if views != 4:
            return [x] + [from_view(x, bits) for bits in range(1, views)]
        one, two = from_view(x, 1), from_view(x, 2)
        first, second = one[:part], two[part:]
        if x.shape[0] > rows_piece:
            first = jnp.concatenate([first, one[rows_piece:]], axis=0)
        return [x, one, two, from_view(first, 2), from_view(second, 1)]

    def own_rows(volume):
        return lax.dynamic_slice_in_dim(volume, view_id * rows_piece, rows_piece, axis=1)

    first_piece = jnp.transpose(own_rows(estimate).astype(half), (1, 0, 2))
    first_piece, volume, data = lax.optimization_barrier((first_piece, estimate, views_data[0]))
    far_blocks = share(far(first_piece))
    bottom, top = data[:REACH], data[core - REACH :]
    to_far, to_near = jnp.where(even, bottom, top), jnp.where(even, top, bottom)
    measured = (far(to_far), data, near(to_near))
    start = jnp.transpose(volume.astype(half), (1, 0, 2))
    blocks = [far_blocks, [start], [near(start)]]

    chosen = (jnp.arange(kernels_count, dtype=jnp.int32) == psf_index[0]).astype(jnp.float32)
    taps = jnp.einsum("k,kat->at", chosen, psf_bank.astype(jnp.float32))
    cores = jnp.arange(core, dtype=jnp.int32) + MARGIN
    below, above = jnp.where(even, 0, MARGIN + core), jnp.where(even, MARGIN + core, 0)
    deep = jnp.arange(MARGIN, dtype=jnp.int32)
    position = jnp.concatenate([deep + below, cores, deep + above])
    low_reach, high_reach = MARGIN - REACH, MARGIN + core
    thin = jnp.arange(REACH, dtype=jnp.int32)
    wanted = jnp.concatenate(
        [
            thin + jnp.where(even, low_reach, high_reach),
            cores,
            thin + jnp.where(even, high_reach, low_reach),
        ]
    )

    def inside(k):
        global_pos = tile_id * core - MARGIN + k
        held = (k >= MARGIN - margin_extent[0, 0]) & (k < MARGIN + core + margin_extent[0, 1])
        return held & (global_pos >= 0) & (global_pos < core * tiles)

    natural = jnp.arange(rows, dtype=jnp.int32)
    held = ((natural // rows_piece) ^ view_id) * rows_piece + natural % rows_piece
    columns = jnp.arange(cols, dtype=jnp.int32)
    z_band = jnp.where(inside(position)[None, :], band(taps[0], wanted, position), 0.0).astype(half)
    z_back = band(taps[0], wanted, cores).T.astype(half)
    y_band = band(taps[1], natural, held).astype(half)
    y_back = y_band.T
    x_back = band(taps[2], columns, columns).astype(half)
    x_band = x_back.T
    mask = inside(wanted).astype(jnp.int32)

    here = view_id.astype(jnp.int32).reshape(1)
    bands = (z_band, z_back, y_band, y_back, x_band, x_back)
    for it in range(ITERS):
        codes = list(sweep(here, mask, pieces, blocks, measured, bands, views))
        if it == 0:
            volume, codes[0] = lax.optimization_barrier((estimate, codes[0]))
            mine = jnp.transpose(own_rows(volume), (1, 0, 2))
        arrived = [codes[0]] + [from_view(codes[bits], bits) for bits in range(1, views)]
        if it + 1 < ITERS:
            mine, rounded = update(arrived, mine, False)
            own = share(rounded)
            blocks = [[far(x) for x in own], own, [near(x) for x in own]]
        else:
            (code,) = update(arrived, mine, True)
    return gather(here, pieces, share(code), rows, views)


def solution(mesh):
    return jax.shard_map(
        on_device,
        mesh=mesh,
        in_specs=(
            P("tile", None, None),
            P("view", "tile", None, None),
            P(),
            P("view"),
            P("tile", None),
        ),
        out_specs=P("tile", None, None),
        check_vma=False,
    )
```

```python
import functools

import jax
import jax.numpy as jnp
from jax import lax
from jax.experimental import pallas as pl
from jax.experimental.pallas import tpu as pltpu
from jax.sharding import PartitionSpec as P

MARGIN = 32
ITERS = 2
REACH = 16
LANES = 128
GROUP = 16
UNROLL = 32
PAD = 8
STEPS = 8.0
LATE = 1
ROOM = 32768.0 / 32000.0
SMALL = 1e-30
VMEM_LIMIT = 56 * 1024 * 1024
ANY = pl.BlockSpec(memory_space=pl.ANY)
VMEM = pl.BlockSpec(memory_space=pltpu.VMEM)
SMEM = pl.BlockSpec(memory_space=pltpu.SMEM)


def dot32(a, b):
    return jnp.dot(a, b, preferred_element_type=jnp.float32)


def halves(value):
    return [value[:, h * LANES : (h + 1) * LANES] for h in range(value.shape[1] // LANES)]


def encode(values):
    top = jnp.maximum(jnp.max(jnp.abs(values), axis=0, keepdims=True), jnp.float32(SMALL))
    power = jnp.ceil(jnp.log2(top * jnp.float32(ROOM)) * jnp.float32(STEPS))
    code = jnp.round(values * jnp.exp2(15.0 - power * jnp.float32(1.0 / STEPS)))
    return code.astype(jnp.int32).astype(jnp.int16), power


def scale_of(powers):
    return jnp.exp2(powers.astype(jnp.float32) * jnp.float32(1.0 / STEPS) - 15.0)


def put_powers(slab_ref, powers):
    depth, count = slab_ref.shape[0], powers.shape[0]
    slab_ref[0:count, :] = powers.astype(jnp.int32).astype(jnp.int16)
    if count < depth:
        slab_ref[count:depth, :] = jnp.zeros((depth - count, powers.shape[1]), jnp.int16)


def sweep_kernel(plan, *refs):
    pieces, shares, pieces_out, core, rows, cols = plan
    refs = list(refs)
    take = lambda n: [refs.pop(0) for _ in range(n)]
    view_ref, mask_ref = take(2)
    sources = [take(n) for n in shares]
    data_sources = take(3)
    z_band, z_back, y_band, y_back, x_band, x_back = take(6)
    outs = take(pieces_out)
    block, measured, by_plane, by_row, codes, powers, in_sem, data_sem, out_sem = refs
    depths = core + 2 * REACH
    lane_parts = cols // LANES
    plane_rows, row_depths = rows + PAD, depths + PAD
    rows_out = rows // pieces_out
    unroll_out = min(UNROLL, rows_out)

    def block_copies(index):
        bits, offset, count = pieces[index]
        copies = []
        for part, given in enumerate(sources):
            if len(given) == 1:
                first = (view_ref[0] ^ bits) * rows_out + offset
                source = given[0].at[pl.ds(first, count)]
            else:
                source = given[index]
            target = block.at[pl.ds(bits * rows_out + offset, count), pl.ds(part * core, core)]
            copies.append(pltpu.make_async_copy(source, target, in_sem.at[part, index]))
        return copies

    data_copies = []
    for step in range(depths // GROUP):
        k = step * GROUP
        which, first = (0, 0) if k < REACH else (1, k - REACH) if k < REACH + core else (2, 0)
        data_copies.append(
            pltpu.make_async_copy(
                data_sources[which].at[pl.ds(first, GROUP)],
                measured.at[pl.ds(k, GROUP)],
                data_sem.at[step],
            )
        )
    for index in range(len(pieces)):
        for copy in block_copies(index):
            copy.start()

    for index, (bits, offset, count) in enumerate(pieces):
        for copy in block_copies(index):
            copy.wait()
        if index == LATE:
            for copy in data_copies:
                copy.start()
        for y in range(bits * rows_out + offset, bits * rows_out + offset + count):
            for h, part in enumerate(halves(dot32(z_band[...], block[y]))):
                by_plane[h, pl.ds(y, depths, stride=plane_rows), :] = part

    def planes(step, carry):
        arriving = measured.at[pl.ds(step * GROUP, GROUP)]
        pltpu.make_async_copy(arriving, arriving, data_sem.at[step]).wait()
        passed = []
        for g in range(GROUP):
            start = pl.multiple_of((step * GROUP + g) * plane_rows, PAD)
            plane = jnp.concatenate(
                [by_plane[h, pl.ds(start, rows), :].astype(jnp.bfloat16) for h in range(lane_parts)],
                axis=1,
            )
            passed.append(dot32(y_band[...], plane).astype(jnp.bfloat16))
        blurred = dot32(jnp.concatenate(passed, axis=0), x_band[...])
        ratios = []
        for g in range(GROUP):
            k = step * GROUP + g
            inside = mask_ref[k] > 0
            data = measured[k].astype(jnp.float32)
            under = jnp.where(inside, blurred[g * rows : (g + 1) * rows], jnp.float32(1.0))
            ratios.append(jnp.where(inside, data / under, jnp.float32(0.0)).astype(jnp.bfloat16))
        back = dot32(jnp.concatenate(ratios, axis=0), x_back[...]).astype(jnp.bfloat16)
        for g in range(GROUP):
            out = dot32(y_back[...], back[g * rows : (g + 1) * rows])
            for h, part in enumerate(halves(out)):
                by_row[h, pl.ds(step * GROUP + g, rows, stride=row_depths), :] = part
        return carry

    lax.fori_loop(0, depths // GROUP, planes, 0)

    out_copies = []
    for p in range(pieces_out):

        def z_return(step, carry, p=p):
            for u in range(unroll_out):
                y = step * unroll_out + u
                start = pl.multiple_of((p * rows_out + y) * row_depths, PAD)
                column = jnp.concatenate(
                    [by_row[h, pl.ds(start, depths), :].astype(jnp.bfloat16) for h in range(lane_parts)],
                    axis=1,
                )
                code, power = encode(dot32(z_back[...], column))
                codes[p, y] = code
                powers[pl.ds(y, 1), :] = power
            return carry

        lax.fori_loop(0, rows_out // unroll_out, z_return, 0)
        put_powers(codes.at[p, rows_out], powers[...])
        copy = pltpu.make_async_copy(codes.at[p], outs[p], out_sem.at[p])
        copy.start()
        out_copies.append(copy)
    for copy in out_copies:
        copy.wait()


def sweep(view_id, mask, pieces, blocks, measured, bands, pieces_out):
    core, (rows, cols) = measured[1].shape[0], measured[1].shape[1:]
    depths = core + 2 * REACH
    rows_out = rows // pieces_out
    shares = tuple(len(part) for part in blocks)
    flat = [piece for part in blocks for piece in part]
    return pl.pallas_call(
        functools.partial(sweep_kernel, (pieces, shares, pieces_out, core, rows, cols)),
        out_shape=[jax.ShapeDtypeStruct((rows_out + 1, core, cols), jnp.int16)] * pieces_out,
        in_specs=[SMEM] * 2 + [ANY] * (len(flat) + 3) + [VMEM] * 6,
        out_specs=[ANY] * pieces_out,
        scratch_shapes=[
            pltpu.VMEM((rows, 3 * core, cols), jnp.bfloat16),
            pltpu.VMEM((depths, rows, cols), jnp.bfloat16),
            pltpu.VMEM((cols // LANES, depths * (rows + PAD), LANES), jnp.float32),
            pltpu.VMEM((cols // LANES, rows * (depths + PAD), LANES), jnp.float32),
            pltpu.VMEM((pieces_out, rows_out + 1, core, cols), jnp.int16),
            pltpu.VMEM((rows_out, cols), jnp.float32),
            pltpu.SemaphoreType.DMA((3, len(pieces))),
            pltpu.SemaphoreType.DMA((depths // GROUP,)),
            pltpu.SemaphoreType.DMA((pieces_out,)),
        ],
        compiler_params=pltpu.CompilerParams(vmem_limit_bytes=VMEM_LIMIT),
        name="sweep",
    )(view_id, mask, *flat, *measured, *bands)


def update_kernel(last, views, *refs):
    codes, mine, outs = refs[:views], refs[views], refs[views + 1 :]
    count = mine.shape[0]
    scales = [scale_of(code[count][0:count]) for code in codes]
    powers = []
    for y in range(count):
        total = sum(
            code[y].astype(jnp.float32) * scale[y : y + 1] for code, scale in zip(codes, scales)
        )
        value = mine[y] * total * jnp.float32(1.0 / views)
        if last:
            outs[0][y], power = encode(value)
            powers.append(power)
        else:
            outs[0][y] = value
            outs[1][y] = value.astype(jnp.bfloat16)
    if last:
        put_powers(outs[0].at[count], jnp.concatenate(powers, axis=0))


def update(codes, mine, last):
    views = len(codes)
    if last:
        shapes = [jax.ShapeDtypeStruct(codes[0].shape, jnp.int16)]
    else:
        shapes = [jax.ShapeDtypeStruct(mine.shape, t) for t in (jnp.float32, jnp.bfloat16)]
    return pl.pallas_call(
        functools.partial(update_kernel, last, views),
        out_shape=shapes,
        in_specs=[VMEM] * (views + 1),
        out_specs=[VMEM] * len(shapes),
        compiler_params=pltpu.CompilerParams(vmem_limit_bytes=VMEM_LIMIT),
        name="update",
    )(*codes, mine)


def gather_kernel(pieces, rows_piece, core, rows, cols, *refs):
    n = len(pieces)
    view_ref, codes = refs[0], refs[1 : n + 1]
    out, planes, sem = refs[-3:]
    plane_rows = rows + PAD
    copies = []
    for index, (code, (bits, offset, count)) in enumerate(zip(codes, pieces)):
        base = pl.multiple_of((view_ref[0] ^ bits) * rows_piece + offset, PAD)
        scale = scale_of(code[count][0:rows_piece])
        for y in range(count):
            value = code[y].astype(jnp.float32) * scale[offset + y : offset + y + 1]
            for h, part in enumerate(halves(value)):
                planes[h, pl.ds(base + y, core, stride=plane_rows), :] = part
        for h in range(cols // LANES):
            for z in range(core):
                copy = pltpu.make_async_copy(
                    planes.at[h, pl.ds(pl.multiple_of(z * plane_rows + base, PAD), count)],
                    out.at[z, pl.ds(base, count), pl.ds(h * LANES, LANES)],
                    sem.at[index, h, z],
                )
                copy.start()
                copies.append(copy)
    for copy in copies:
        copy.wait()


def gather(view_id, pieces, codes, rows, views, tile=None):
    core, cols = codes[0].shape[1:]
    given = [] if tile is None else [tile]
    return pl.pallas_call(
        functools.partial(gather_kernel, pieces, rows // views, core, rows, cols),
        out_shape=jax.ShapeDtypeStruct((core, rows, cols), jnp.float32),
        in_specs=[SMEM] + [VMEM] * len(codes) + [ANY] * len(given),
        out_specs=ANY,
        scratch_shapes=[
            pltpu.VMEM((cols // LANES, core * (rows + PAD), LANES), jnp.float32),
            pltpu.SemaphoreType.DMA((len(codes), cols // LANES, core)),
        ],
        input_output_aliases={} if tile is None else {1 + len(codes): 0},
        compiler_params=pltpu.CompilerParams(vmem_limit_bytes=VMEM_LIMIT),
        name="gather",
    )(view_id, *codes, *given)


def band(taps, row_index, col_index):
    count = taps.shape[0]
    offsets = col_index[None, :] - row_index[:, None] + (count - 1) // 2
    chosen = offsets[None, :, :] == jnp.arange(count, dtype=jnp.int32)[:, None, None]
    return jnp.sum(jnp.where(chosen, taps[:, None, None], jnp.float32(0.0)), axis=0)


def on_device(estimate, views_data, psf_bank, psf_index, margin_extent):
    core, rows, cols = estimate.shape
    kernels_count = psf_bank.shape[0]
    tiles = lax.axis_size("tile")
    views = lax.axis_size("view")
    tile_id = lax.axis_index("tile")
    view_id = lax.axis_index("view")
    rows_piece = rows // views
    half = jnp.bfloat16

    near_pairs = [(t, t ^ 1) for t in range(tiles)]
    far_pairs = [(t, ((t + 1) ^ 1) - 1) for t in range(1, tiles - 1)]
    even = tile_id % 2 == 0

    def far(x):
        return lax.ppermute(x, "tile", far_pairs)

    def near(x):
        return lax.ppermute(x, "tile", near_pairs)

    def from_view(x, bits):
        return lax.ppermute(x, "view", [(v, v ^ bits) for v in range(views)])

    part = rows_piece // 2
    if views == 4:
        pieces = ((0, 0, rows_piece), (1, 0, rows_piece), (2, 0, rows_piece), (3, 0, part), (3, part, part))
    else:
        pieces = tuple((bits, 0, rows_piece) for bits in range(views))

    def share(x, send=None):
        send = send or (lambda y: y)
        sent = [send(x)]
        if views != 4:
            every = [x] + [from_view(x, bits) for bits in range(1, views)]
            return every, sent + [send(y) for y in every[1:]]
        one, two = from_view(x, 1), from_view(x, 2)
        sent += [send(one), send(two)]
        first, second = one[:part], two[part:]
        if x.shape[0] > rows_piece:
            first = jnp.concatenate([first, one[rows_piece:]], axis=0)
        rest = [from_view(first, 2), from_view(second, 1)]
        return [x, one, two, *rest], sent + [send(y) for y in rest]

    def own_rows(volume):
        return lax.dynamic_slice_in_dim(volume, view_id * rows_piece, rows_piece, axis=1)

    first_piece = jnp.transpose(own_rows(estimate).astype(half), (1, 0, 2))
    first_piece, volume, data = lax.optimization_barrier((first_piece, estimate, views_data[0]))
    far_piece = far(first_piece)
    bottom, top = data[:REACH], data[core - REACH :]
    to_far, to_near = jnp.where(even, bottom, top), jnp.where(even, top, bottom)
    far_piece, to_far, psf_bank = lax.optimization_barrier((far_piece, to_far, psf_bank))
    far_blocks, _ = share(far_piece)
    measured = (far(to_far), data, near(to_near))
    start = jnp.transpose(volume.astype(half), (1, 0, 2))
    blocks = [far_blocks, [start], [near(start)]]

    chosen = (jnp.arange(kernels_count, dtype=jnp.int32) == psf_index[0]).astype(jnp.float32)
    taps = jnp.einsum("k,kat->at", chosen, psf_bank.astype(jnp.float32))
    cores = jnp.arange(core, dtype=jnp.int32) + MARGIN
    below, above = jnp.where(even, 0, MARGIN + core), jnp.where(even, MARGIN + core, 0)
    deep = jnp.arange(MARGIN, dtype=jnp.int32)
    position = jnp.concatenate([deep + below, cores, deep + above])
    low_reach, high_reach = MARGIN - REACH, MARGIN + core
    thin = jnp.arange(REACH, dtype=jnp.int32)
    wanted = jnp.concatenate(
        [
            thin + jnp.where(even, low_reach, high_reach),
            cores,
            thin + jnp.where(even, high_reach, low_reach),
        ]
    )

    def inside(k):
        global_pos = tile_id * core - MARGIN + k
        held = (k >= MARGIN - margin_extent[0, 0]) & (k < MARGIN + core + margin_extent[0, 1])
        return held & (global_pos >= 0) & (global_pos < core * tiles)

    natural = jnp.arange(rows, dtype=jnp.int32)
    held = ((natural // rows_piece) ^ view_id) * rows_piece + natural % rows_piece
    columns = jnp.arange(cols, dtype=jnp.int32)
    z_band = jnp.where(inside(position)[None, :], band(taps[0], wanted, position), 0.0).astype(half)
    z_back = band(taps[0], wanted, cores).T.astype(half)
    y_band = band(taps[1], natural, held).astype(half)
    y_back = y_band.T
    x_back = band(taps[2], columns, columns).astype(half)
    x_band = x_back.T
    mask = inside(wanted).astype(jnp.int32)

    here = view_id.astype(jnp.int32).reshape(1)
    bands = (z_band, z_back, y_band, y_back, x_band, x_back)
    for it in range(ITERS):
        codes = list(sweep(here, mask, pieces, blocks, measured, bands, views))
        if it == 0:
            volume, codes[0] = lax.optimization_barrier((estimate, codes[0]))
            mine = jnp.transpose(own_rows(volume), (1, 0, 2))
        arrived = [codes[0]] + [from_view(codes[bits], bits) for bits in range(1, views)]
        if it + 1 < ITERS:
            mine, rounded = update(arrived, mine, False)
            own, fars = share(rounded, far)
            blocks = [fars, own, [near(x) for x in own]]
        else:
            (code,) = update(arrived, mine, True)
    codes, _ = share(code)
    early = min(3, len(codes))
    tile = gather(here, pieces[:early], codes[:early], rows, views)
    if early == len(codes):
        return tile
    return gather(here, pieces[early:], codes[early:], rows, views, tile)


def solution(mesh):
    return jax.shard_map(
        on_device,
        mesh=mesh,
        in_specs=(
            P("tile", None, None),
            P("view", "tile", None, None),
            P(),
            P("view"),
            P("tile", None),
        ),
        out_specs=P("tile", None, None),
        check_vma=False,
    )
```

```python
import functools

import jax
import jax.numpy as jnp
from jax import lax
from jax.experimental import pallas as pl
from jax.experimental.pallas import tpu as pltpu
from jax.sharding import PartitionSpec as P

MARGIN = 32
ITERS = 2
REACH = 16
LANES = 128
GROUP = 16
UNROLL = 32
PAD = 8
STEPS = 8.0
LATE = 1
BLOCKS = 4
ROOM = 32768.0 / 32000.0
SMALL = 1e-30
VMEM_LIMIT = 56 * 1024 * 1024
ANY = pl.BlockSpec(memory_space=pltpu.HBM)
VMEM = pl.BlockSpec(memory_space=pltpu.VMEM)
SMEM = pl.BlockSpec(memory_space=pltpu.SMEM)


def dot32(a, b):
    return jnp.dot(a, b, preferred_element_type=jnp.float32)


def halves(value):
    return [value[:, h * LANES : (h + 1) * LANES] for h in range(value.shape[1] // LANES)]


def encode(values):
    top = jnp.maximum(jnp.max(jnp.abs(values), axis=0, keepdims=True), jnp.float32(SMALL))
    power = jnp.ceil(jnp.log2(top * jnp.float32(ROOM)) * jnp.float32(STEPS))
    code = jnp.round(values * jnp.exp2(15.0 - power * jnp.float32(1.0 / STEPS)))
    return code.astype(jnp.int32).astype(jnp.int16), power


def scale_of(powers):
    return jnp.exp2(powers.astype(jnp.float32) * jnp.float32(1.0 / STEPS) - 15.0)


def put_powers(slab_ref, powers):
    depth, count = slab_ref.shape[0], powers.shape[0]
    slab_ref[0:count, :] = powers.astype(jnp.int32).astype(jnp.int16)
    if count < depth:
        slab_ref[count:depth, :] = jnp.zeros((depth - count, powers.shape[1]), jnp.int16)


def sweep_kernel(plan, *refs):
    pieces, shares, pieces_out, core, rows, cols = plan
    refs = list(refs)
    take = lambda n: [refs.pop(0) for _ in range(n)]
    view_ref, mask_ref = take(2)
    sources = [take(n) for n in shares]
    data_sources = take(3)
    z_band, z_back, y_band, y_back, x_band, x_back = take(6)
    outs = take(pieces_out)
    block, measured, by_plane, by_row, codes, powers, in_sem, data_sem, out_sem = refs
    depths = core + 2 * REACH
    lane_parts = cols // LANES
    plane_rows, row_depths = rows + PAD, depths + PAD
    rows_out = rows // pieces_out
    unroll_out = min(UNROLL, rows_out)

    def block_copies(index):
        bits, offset, count = pieces[index]
        copies = []
        for part, given in enumerate(sources):
            if len(given) == pieces_out and len(pieces) != pieces_out:
                source = given[bits].at[pl.ds(offset, count)]
            elif len(given) == 1:
                first = (view_ref[0] ^ bits) * rows_out + offset
                source = given[0].at[pl.ds(first, count)]
            else:
                source = given[index]
            target = block.at[pl.ds(bits * rows_out + offset, count), pl.ds(part * core, core)]
            copies.append(pltpu.make_async_copy(source, target, in_sem.at[part, index]))
        return copies

    data_copies = []
    for step in range(depths // GROUP):
        k = step * GROUP
        which, first = (0, 0) if k < REACH else (1, k - REACH) if k < REACH + core else (2, 0)
        data_copies.append(
            pltpu.make_async_copy(
                data_sources[which].at[pl.ds(first, GROUP)],
                measured.at[pl.ds(k, GROUP)],
                data_sem.at[step],
            )
        )
    for index in range(len(pieces)):
        for copy in block_copies(index):
            copy.start()

    for index, (bits, offset, count) in enumerate(pieces):
        for copy in block_copies(index):
            copy.wait()
        if index == LATE:
            for copy in data_copies:
                copy.start()
        for y in range(bits * rows_out + offset, bits * rows_out + offset + count):
            for h, part in enumerate(halves(dot32(z_band[...], block[y]))):
                by_plane[h, pl.ds(y, depths, stride=plane_rows), :] = part

    def planes(step, carry):
        arriving = measured.at[pl.ds(step * GROUP, GROUP)]
        pltpu.make_async_copy(arriving, arriving, data_sem.at[step]).wait()
        passed = []
        for g in range(GROUP):
            start = pl.multiple_of((step * GROUP + g) * plane_rows, PAD)
            plane = jnp.concatenate(
                [by_plane[h, pl.ds(start, rows), :].astype(jnp.bfloat16) for h in range(lane_parts)],
                axis=1,
            )
            passed.append(dot32(y_band[...], plane).astype(jnp.bfloat16))
        blurred = dot32(jnp.concatenate(passed, axis=0), x_band[...])
        ratios = []
        for g in range(GROUP):
            k = step * GROUP + g
            inside = mask_ref[k] > 0
            data = measured[k].astype(jnp.float32)
            under = jnp.where(inside, blurred[g * rows : (g + 1) * rows], jnp.float32(1.0))
            ratios.append(jnp.where(inside, data / under, jnp.float32(0.0)).astype(jnp.bfloat16))
        back = dot32(jnp.concatenate(ratios, axis=0), x_back[...]).astype(jnp.bfloat16)
        for g in range(GROUP):
            out = dot32(y_back[...], back[g * rows : (g + 1) * rows])
            for h, part in enumerate(halves(out)):
                by_row[h, pl.ds(step * GROUP + g, rows, stride=row_depths), :] = part
        return carry

    lax.fori_loop(0, depths // GROUP, planes, 0)

    out_copies = []
    for p in range(pieces_out):

        def z_return(step, carry, p=p):
            for u in range(unroll_out):
                y = step * unroll_out + u
                start = pl.multiple_of((p * rows_out + y) * row_depths, PAD)
                column = jnp.concatenate(
                    [by_row[h, pl.ds(start, depths), :].astype(jnp.bfloat16) for h in range(lane_parts)],
                    axis=1,
                )
                code, power = encode(dot32(z_back[...], column))
                codes[p, y] = code
                powers[pl.ds(y, 1), :] = power
            return carry

        lax.fori_loop(0, rows_out // unroll_out, z_return, 0)
        put_powers(codes.at[p, rows_out], powers[...])
        copy = pltpu.make_async_copy(codes.at[p], outs[p], out_sem.at[p])
        copy.start()
        out_copies.append(copy)
    for copy in out_copies:
        copy.wait()


def sweep(view_id, mask, pieces, blocks, measured, bands, pieces_out):
    core, (rows, cols) = measured[1].shape[0], measured[1].shape[1:]
    depths = core + 2 * REACH
    rows_out = rows // pieces_out
    shares = tuple(len(part) for part in blocks)
    flat = [piece for part in blocks for piece in part]
    return pl.pallas_call(
        functools.partial(sweep_kernel, (pieces, shares, pieces_out, core, rows, cols)),
        out_shape=[jax.ShapeDtypeStruct((rows_out + 1, core, cols), jnp.int16)] * pieces_out,
        in_specs=[SMEM] * 2 + [ANY] * (len(flat) + 3) + [VMEM] * 6,
        out_specs=[ANY] * pieces_out,
        scratch_shapes=[
            pltpu.VMEM((rows, 3 * core, cols), jnp.bfloat16),
            pltpu.VMEM((depths, rows, cols), jnp.bfloat16),
            pltpu.VMEM((cols // LANES, depths * (rows + PAD), LANES), jnp.float32),
            pltpu.VMEM((cols // LANES, rows * (depths + PAD), LANES), jnp.float32),
            pltpu.VMEM((pieces_out, rows_out + 1, core, cols), jnp.int16),
            pltpu.VMEM((rows_out, cols), jnp.float32),
            pltpu.SemaphoreType.DMA((3, len(pieces))),
            pltpu.SemaphoreType.DMA((depths // GROUP,)),
            pltpu.SemaphoreType.DMA((pieces_out,)),
        ],
        compiler_params=pltpu.CompilerParams(vmem_limit_bytes=VMEM_LIMIT),
        name="sweep",
    )(view_id, mask, *flat, *measured, *bands)


def update_kernel(last, views, *refs):
    count, kinds = refs[views].shape[0], 1 if last else 2
    given, outs = refs[: views + 1], refs[views + 1 : views + 1 + kinds]
    held, made = refs[views + 1 + kinds : 2 * views + 2 + kinds], refs[2 * views + 2 + kinds : -3]
    slab_sem, in_sem, out_sem = refs[-3:]
    codes, mine = held[:views], held[views]
    size = count // BLOCKS

    def loads(c):
        rows = pl.ds(c * size, size)
        pairs = enumerate(zip(given, held))
        return [pltpu.make_async_copy(a.at[rows], b.at[rows], in_sem.at[c, i]) for i, (a, b) in pairs]

    def stores(c):
        rows = pl.ds(c * size, size + 1 if last and c == BLOCKS - 1 else size)
        pairs = enumerate(zip(made, outs))
        return [pltpu.make_async_copy(a.at[rows], b.at[rows], out_sem.at[c, i]) for i, (a, b) in pairs]

    slabs = [
        pltpu.make_async_copy(given[v].at[count], codes[v].at[count], slab_sem.at[v])
        for v in range(views)
    ]
    for copy in slabs + [copy for c in range(BLOCKS) for copy in loads(c)]:
        copy.start()
    for copy in slabs:
        copy.wait()
    scales = [scale_of(code[count][0:count]) for code in codes]
    powers = []
    for c in range(BLOCKS):
        for copy in loads(c):
            copy.wait()
        for y in range(c * size, c * size + size):
            total = sum(
                code[y].astype(jnp.float32) * scale[y : y + 1] for code, scale in zip(codes, scales)
            )
            value = mine[y] * total * jnp.float32(1.0 / views)
            if last:
                made[0][y], power = encode(value)
                powers.append(power)
            else:
                made[0][y] = value
                made[1][y] = value.astype(jnp.bfloat16)
        if last and c == BLOCKS - 1:
            put_powers(made[0].at[count], jnp.concatenate(powers, axis=0))
        for copy in stores(c):
            copy.start()
    for c in range(BLOCKS):
        for copy in stores(c):
            copy.wait()


def update(codes, mine, last):
    views = len(codes)
    if last:
        shapes = [jax.ShapeDtypeStruct(codes[0].shape, jnp.int16)]
    else:
        shapes = [jax.ShapeDtypeStruct(mine.shape, t) for t in (jnp.float32, jnp.bfloat16)]
    return pl.pallas_call(
        functools.partial(update_kernel, last, views),
        out_shape=shapes,
        in_specs=[ANY] * (views + 1),
        out_specs=[ANY] * len(shapes),
        scratch_shapes=[pltpu.VMEM(x.shape, x.dtype) for x in (*codes, mine, *shapes)]
        + [
            pltpu.SemaphoreType.DMA((views,)),
            pltpu.SemaphoreType.DMA((BLOCKS, views + 1)),
            pltpu.SemaphoreType.DMA((BLOCKS, len(shapes))),
        ],
        compiler_params=pltpu.CompilerParams(vmem_limit_bytes=VMEM_LIMIT),
        name="update",
    )(*codes, mine)


def gather_kernel(pieces, rows_piece, core, rows, cols, *refs):
    n = len(pieces)
    view_ref, codes = refs[0], refs[1 : n + 1]
    out, planes, sem = refs[-3:]
    plane_rows = rows + PAD
    copies = []
    for index, (code, (bits, offset, count)) in enumerate(zip(codes, pieces)):
        base = pl.multiple_of((view_ref[0] ^ bits) * rows_piece + offset, PAD)
        scale = scale_of(code[count][0:rows_piece])
        for y in range(count):
            value = code[y].astype(jnp.float32) * scale[offset + y : offset + y + 1]
            for h, part in enumerate(halves(value)):
                planes[h, pl.ds(base + y, core, stride=plane_rows), :] = part
        for h in range(cols // LANES):
            copy = pltpu.make_async_copy(
                planes.at[h].reshape(core, plane_rows, LANES).at[:, pl.ds(base, count)],
                out.at[:, pl.ds(base, count), pl.ds(h * LANES, LANES)],
                sem.at[index, h],
            )
            copy.start()
            copies.append(copy)
    for copy in copies:
        copy.wait()


def gather(view_id, pieces, codes, rows, views, tile=None):
    core, cols = codes[0].shape[1:]
    given = [] if tile is None else [tile]
    return pl.pallas_call(
        functools.partial(gather_kernel, pieces, rows // views, core, rows, cols),
        out_shape=jax.ShapeDtypeStruct((core, rows, cols), jnp.float32),
        in_specs=[SMEM] + [VMEM] * len(codes) + [ANY] * len(given),
        out_specs=ANY,
        scratch_shapes=[
            pltpu.VMEM((cols // LANES, core * (rows + PAD), LANES), jnp.float32),
            pltpu.SemaphoreType.DMA((len(codes), cols // LANES)),
        ],
        input_output_aliases={} if tile is None else {1 + len(codes): 0},
        compiler_params=pltpu.CompilerParams(vmem_limit_bytes=VMEM_LIMIT),
        name="gather",
    )(view_id, *codes, *given)


def band(taps, row_index, col_index):
    count = taps.shape[0]
    offsets = col_index[None, :] - row_index[:, None] + (count - 1) // 2
    chosen = offsets[None, :, :] == jnp.arange(count, dtype=jnp.int32)[:, None, None]
    return jnp.sum(jnp.where(chosen, taps[:, None, None], jnp.float32(0.0)), axis=0)


def on_device(estimate, views_data, psf_bank, psf_index, margin_extent):
    core, rows, cols = estimate.shape
    kernels_count = psf_bank.shape[0]
    tiles = lax.axis_size("tile")
    views = lax.axis_size("view")
    tile_id = lax.axis_index("tile")
    view_id = lax.axis_index("view")
    rows_piece = rows // views
    half = jnp.bfloat16

    near_pairs = [(t, t ^ 1) for t in range(tiles)]
    far_pairs = [(t, ((t + 1) ^ 1) - 1) for t in range(1, tiles - 1)]
    even = tile_id % 2 == 0

    def far(x):
        return lax.ppermute(x, "tile", far_pairs)

    def near(x):
        return lax.ppermute(x, "tile", near_pairs)

    def from_view(x, bits):
        return lax.ppermute(x, "view", [(v, v ^ bits) for v in range(views)])

    part = rows_piece // 2
    if views == 4:
        pieces = ((0, 0, rows_piece), (1, 0, rows_piece), (2, 0, rows_piece), (3, 0, part), (3, part, part))
    else:
        pieces = tuple((bits, 0, rows_piece) for bits in range(views))

    def share(x, send=None):
        send = send or (lambda y: y)
        sent = [send(x)]
        if views != 4:
            every = [x] + [from_view(x, bits) for bits in range(1, views)]
            return every, sent + [send(y) for y in every[1:]]
        one, two = from_view(x, 1), from_view(x, 2)
        sent += [send(one), send(two)]
        first, second = one[:part], two[part:]
        if x.shape[0] > rows_piece:
            first = jnp.concatenate([first, one[rows_piece:]], axis=0)
        rest = [from_view(first, 2), from_view(second, 1)]
        return [x, one, two, *rest], sent + [send(jnp.concatenate(rest, axis=0))]

    def own_rows(volume):
        return lax.dynamic_slice_in_dim(volume, view_id * rows_piece, rows_piece, axis=1)

    first_piece = jnp.transpose(own_rows(estimate).astype(half), (1, 0, 2))
    first_piece, volume, data = lax.optimization_barrier((first_piece, estimate, views_data[0]))
    far_piece = far(first_piece)
    bottom, top = data[:REACH], data[core - REACH :]
    to_far, to_near = jnp.where(even, bottom, top), jnp.where(even, top, bottom)
    far_piece, to_far, psf_bank = lax.optimization_barrier((far_piece, to_far, psf_bank))
    far_blocks, _ = share(far_piece)
    measured = (far(to_far), data, near(to_near))
    start = jnp.transpose(volume.astype(half), (1, 0, 2))
    blocks = [far_blocks, [start], [near(start)]]

    chosen = (jnp.arange(kernels_count, dtype=jnp.int32) == psf_index[0]).astype(jnp.float32)
    taps = jnp.einsum("k,kat->at", chosen, psf_bank.astype(jnp.float32))
    cores = jnp.arange(core, dtype=jnp.int32) + MARGIN
    below, above = jnp.where(even, 0, MARGIN + core), jnp.where(even, MARGIN + core, 0)
    deep = jnp.arange(MARGIN, dtype=jnp.int32)
    position = jnp.concatenate([deep + below, cores, deep + above])
    low_reach, high_reach = MARGIN - REACH, MARGIN + core
    thin = jnp.arange(REACH, dtype=jnp.int32)
    wanted = jnp.concatenate(
        [
            thin + jnp.where(even, low_reach, high_reach),
            cores,
            thin + jnp.where(even, high_reach, low_reach),
        ]
    )

    def inside(k):
        global_pos = tile_id * core - MARGIN + k
        held = (k >= MARGIN - margin_extent[0, 0]) & (k < MARGIN + core + margin_extent[0, 1])
        return held & (global_pos >= 0) & (global_pos < core * tiles)

    natural = jnp.arange(rows, dtype=jnp.int32)
    held = ((natural // rows_piece) ^ view_id) * rows_piece + natural % rows_piece
    columns = jnp.arange(cols, dtype=jnp.int32)
    z_band = jnp.where(inside(position)[None, :], band(taps[0], wanted, position), 0.0).astype(half)
    z_back = band(taps[0], wanted, cores).T.astype(half)
    y_band = band(taps[1], natural, held).astype(half)
    y_back = y_band.T
    x_back = band(taps[2], columns, columns).astype(half)
    x_band = x_back.T
    mask = inside(wanted).astype(jnp.int32)

    here = view_id.astype(jnp.int32).reshape(1)
    bands = (z_band, z_back, y_band, y_back, x_band, x_back)
    for it in range(ITERS):
        codes = list(sweep(here, mask, pieces, blocks, measured, bands, views))
        if it == 0:
            volume, codes[0] = lax.optimization_barrier((estimate, codes[0]))
            mine = jnp.transpose(own_rows(volume), (1, 0, 2))
        arrived = [codes[0]] + [from_view(codes[bits], bits) for bits in range(1, views)]
        if it + 1 < ITERS:
            mine, rounded = update(arrived, mine, False)
            own, fars = share(rounded, far)
            blocks = [fars, own, [near(x) for x in lax.optimization_barrier(tuple(own))]]
        else:
            (code,) = update(arrived, mine, True)
    codes, _ = share(code)
    early = min(3, len(codes))
    tile = gather(here, pieces[:early], codes[:early], rows, views)
    if early == len(codes):
        return tile
    return gather(here, pieces[early:], codes[early:], rows, views, tile)


def solution(mesh):
    return jax.shard_map(
        on_device,
        mesh=mesh,
        in_specs=(
            P("tile", None, None),
            P("view", "tile", None, None),
            P(),
            P("view"),
            P("tile", None),
        ),
        out_specs=P("tile", None, None),
        check_vma=False,
    )
```

```python
import functools

import jax
import jax.numpy as jnp
from jax import lax
from jax.experimental import pallas as pl
from jax.experimental.pallas import tpu as pltpu
from jax.sharding import PartitionSpec as P

MARGIN = 32
ITERS = 2
REACH = 16
LANES = 128
GROUP = 16
UNROLL = 32
PAD = 8
STEPS = 8.0
LATE = 1
BLOCKS = 4
ROOM = 32768.0 / 32000.0
SMALL = 1e-30
VMEM_LIMIT = 56 * 1024 * 1024
ANY = pl.BlockSpec(memory_space=pltpu.HBM)
VMEM = pl.BlockSpec(memory_space=pltpu.VMEM)
SMEM = pl.BlockSpec(memory_space=pltpu.SMEM)


def dot32(a, b):
    return jnp.dot(a, b, preferred_element_type=jnp.float32)


def halves(value):
    return [value[:, h * LANES : (h + 1) * LANES] for h in range(value.shape[1] // LANES)]


def encode(values):
    top = jnp.maximum(jnp.max(jnp.abs(values), axis=0, keepdims=True), jnp.float32(SMALL))
    power = jnp.ceil(jnp.log2(top * jnp.float32(ROOM)) * jnp.float32(STEPS))
    code = jnp.round(values * jnp.exp2(15.0 - power * jnp.float32(1.0 / STEPS)))
    return code.astype(jnp.int32).astype(jnp.int16), power


def scale_of(powers):
    return jnp.exp2(powers.astype(jnp.float32) * jnp.float32(1.0 / STEPS) - 15.0)


def put_powers(slab_ref, powers):
    depth, count = slab_ref.shape[0], powers.shape[0]
    slab_ref[0:count, :] = powers.astype(jnp.int32).astype(jnp.int16)
    if count < depth:
        slab_ref[count:depth, :] = jnp.zeros((depth - count, powers.shape[1]), jnp.int16)


def sweep_kernel(plan, *refs):
    pieces, shares, pieces_out, core, rows, cols = plan
    refs = list(refs)
    take = lambda n: [refs.pop(0) for _ in range(n)]
    view_ref, mask_ref = take(2)
    sources = [take(n) for n in shares]
    data_sources = take(3)
    z_band, z_back, y_band, y_back, x_band, x_back = take(6)
    outs = take(pieces_out)
    block, measured, by_plane, by_row, codes, powers, in_sem, data_sem, out_sem = refs
    depths = core + 2 * REACH
    lane_parts = cols // LANES
    plane_rows, row_depths = rows + PAD, depths + PAD
    rows_out = rows // pieces_out
    unroll_out = min(UNROLL, rows_out)

    def block_copies(index):
        bits, offset, count = pieces[index]
        copies = []
        for part, given in enumerate(sources):
            if len(given) == pieces_out and len(pieces) != pieces_out:
                source = given[bits].at[pl.ds(offset, count)]
            elif len(given) == 1:
                first = (view_ref[0] ^ bits) * rows_out + offset
                source = given[0].at[pl.ds(first, count)]
            else:
                source = given[index]
            target = block.at[pl.ds(bits * rows_out + offset, count), pl.ds(part * core, core)]
            copies.append(pltpu.make_async_copy(source, target, in_sem.at[part, index]))
        return copies

    data_copies = []
    for step in range(depths // GROUP):
        k = step * GROUP
        which, first = (0, 0) if k < REACH else (1, k - REACH) if k < REACH + core else (2, 0)
        data_copies.append(
            pltpu.make_async_copy(
                data_sources[which].at[pl.ds(first, GROUP)],
                measured.at[pl.ds(k, GROUP)],
                data_sem.at[step],
            )
        )
    for index in range(len(pieces)):
        for copy in block_copies(index):
            copy.start()

    for index, (bits, offset, count) in enumerate(pieces):
        for copy in block_copies(index):
            copy.wait()
        if index == LATE:
            for copy in data_copies:
                copy.start()
        for y in range(bits * rows_out + offset, bits * rows_out + offset + count):
            for h, part in enumerate(halves(dot32(z_band[...], block[y]))):
                by_plane[h, pl.ds(y, depths, stride=plane_rows), :] = part

    def planes(step, carry):
        arriving = measured.at[pl.ds(step * GROUP, GROUP)]
        pltpu.make_async_copy(arriving, arriving, data_sem.at[step]).wait()
        passed = []
        for g in range(GROUP):
            start = pl.multiple_of((step * GROUP + g) * plane_rows, PAD)
            plane = jnp.concatenate(
                [by_plane[h, pl.ds(start, rows), :].astype(jnp.bfloat16) for h in range(lane_parts)],
                axis=1,
            )
            passed.append(dot32(y_band[...], plane).astype(jnp.bfloat16))
        blurred = dot32(jnp.concatenate(passed, axis=0), x_band[...])
        ratios = []
        for g in range(GROUP):
            k = step * GROUP + g
            inside = mask_ref[k] > 0
            data = measured[k].astype(jnp.float32)
            under = jnp.where(inside, blurred[g * rows : (g + 1) * rows], jnp.float32(1.0))
            ratios.append(jnp.where(inside, data / under, jnp.float32(0.0)).astype(jnp.bfloat16))
        back = dot32(jnp.concatenate(ratios, axis=0), x_back[...]).astype(jnp.bfloat16)
        for g in range(GROUP):
            out = dot32(y_back[...], back[g * rows : (g + 1) * rows])
            for h, part in enumerate(halves(out)):
                by_row[h, pl.ds(step * GROUP + g, rows, stride=row_depths), :] = part
        return carry

    lax.fori_loop(0, depths // GROUP, planes, 0)

    out_copies = []
    for p in range(pieces_out):

        def z_return(step, carry, p=p):
            for u in range(unroll_out):
                y = step * unroll_out + u
                start = pl.multiple_of((p * rows_out + y) * row_depths, PAD)
                column = jnp.concatenate(
                    [by_row[h, pl.ds(start, depths), :].astype(jnp.bfloat16) for h in range(lane_parts)],
                    axis=1,
                )
                code, power = encode(dot32(z_back[...], column))
                codes[p, y] = code
                powers[pl.ds(y, 1), :] = power
            return carry

        lax.fori_loop(0, rows_out // unroll_out, z_return, 0)
        put_powers(codes.at[p, rows_out], powers[...])
        copy = pltpu.make_async_copy(codes.at[p], outs[p], out_sem.at[p])
        copy.start()
        out_copies.append(copy)
    for copy in out_copies:
        copy.wait()


def sweep(view_id, mask, pieces, blocks, measured, bands, pieces_out):
    core, (rows, cols) = measured[1].shape[0], measured[1].shape[1:]
    depths = core + 2 * REACH
    rows_out = rows // pieces_out
    shares = tuple(len(part) for part in blocks)
    flat = [piece for part in blocks for piece in part]
    return pl.pallas_call(
        functools.partial(sweep_kernel, (pieces, shares, pieces_out, core, rows, cols)),
        out_shape=[jax.ShapeDtypeStruct((rows_out + 1, core, cols), jnp.int16)] * pieces_out,
        in_specs=[SMEM] * 2 + [ANY] * (len(flat) + 3) + [VMEM] * 6,
        out_specs=[ANY] * pieces_out,
        scratch_shapes=[
            pltpu.VMEM((rows, 3 * core, cols), jnp.bfloat16),
            pltpu.VMEM((depths, rows, cols), jnp.bfloat16),
            pltpu.VMEM((cols // LANES, depths * (rows + PAD), LANES), jnp.float32),
            pltpu.VMEM((cols // LANES, rows * (depths + PAD), LANES), jnp.float32),
            pltpu.VMEM((pieces_out, rows_out + 1, core, cols), jnp.int16),
            pltpu.VMEM((rows_out, cols), jnp.float32),
            pltpu.SemaphoreType.DMA((3, len(pieces))),
            pltpu.SemaphoreType.DMA((depths // GROUP,)),
            pltpu.SemaphoreType.DMA((pieces_out,)),
        ],
        compiler_params=pltpu.CompilerParams(vmem_limit_bytes=VMEM_LIMIT),
        name="sweep",
    )(view_id, mask, *flat, *measured, *bands)


def update_kernel(last, views, *refs):
    count, kinds = refs[views].shape[0], 1 if last else 2
    given, outs = refs[: views + 1], refs[views + 1 : views + 1 + kinds]
    held, made = refs[views + 1 + kinds : 2 * views + 2 + kinds], refs[2 * views + 2 + kinds : -3]
    slab_sem, in_sem, out_sem = refs[-3:]
    codes, mine = held[:views], held[views]
    size = count // BLOCKS

    def loads(c):
        rows = pl.ds(c * size, size)
        pairs = enumerate(zip(given, held))
        return [pltpu.make_async_copy(a.at[rows], b.at[rows], in_sem.at[c, i]) for i, (a, b) in pairs]

    def stores(c):
        rows = pl.ds(c * size, size + 1 if last and c == BLOCKS - 1 else size)
        pairs = enumerate(zip(made, outs))
        return [pltpu.make_async_copy(a.at[rows], b.at[rows], out_sem.at[c, i]) for i, (a, b) in pairs]

    slabs = [
        pltpu.make_async_copy(given[v].at[count], codes[v].at[count], slab_sem.at[v])
        for v in range(views)
    ]
    for copy in slabs + [copy for c in range(BLOCKS) for copy in loads(c)]:
        copy.start()
    for copy in slabs:
        copy.wait()
    scales = [scale_of(code[count][0:count]) for code in codes]
    powers = []
    for c in range(BLOCKS):
        for copy in loads(c):
            copy.wait()
        for y in range(c * size, c * size + size):
            total = sum(
                code[y].astype(jnp.float32) * scale[y : y + 1] for code, scale in zip(codes, scales)
            )
            value = mine[y] * total * jnp.float32(1.0 / views)
            if last:
                made[0][y], power = encode(value)
                powers.append(power)
            else:
                made[0][y] = value
                made[1][y] = value.astype(jnp.bfloat16)
        if last and c == BLOCKS - 1:
            put_powers(made[0].at[count], jnp.concatenate(powers, axis=0))
        for copy in stores(c):
            copy.start()
    for c in range(BLOCKS):
        for copy in stores(c):
            copy.wait()


def update(codes, mine, last):
    views = len(codes)
    if last:
        shapes = [jax.ShapeDtypeStruct(codes[0].shape, jnp.int16)]
    else:
        shapes = [jax.ShapeDtypeStruct(mine.shape, t) for t in (jnp.float32, jnp.bfloat16)]
    return pl.pallas_call(
        functools.partial(update_kernel, last, views),
        out_shape=shapes,
        in_specs=[ANY] * (views + 1),
        out_specs=[ANY] * len(shapes),
        scratch_shapes=[pltpu.VMEM(x.shape, x.dtype) for x in (*codes, mine, *shapes)]
        + [
            pltpu.SemaphoreType.DMA((views,)),
            pltpu.SemaphoreType.DMA((BLOCKS, views + 1)),
            pltpu.SemaphoreType.DMA((BLOCKS, len(shapes))),
        ],
        compiler_params=pltpu.CompilerParams(vmem_limit_bytes=VMEM_LIMIT),
        name="update",
    )(*codes, mine)


def gather_kernel(pieces, rows_piece, core, rows, cols, *refs):
    n = len(pieces)
    view_ref, codes = refs[0], refs[1 : n + 1]
    out, planes, sem = refs[-3:]
    plane_rows = rows + PAD
    copies = []
    for index, (code, (bits, offset, count)) in enumerate(zip(codes, pieces)):
        base = pl.multiple_of((view_ref[0] ^ bits) * rows_piece + offset, PAD)
        scale = scale_of(code[count][0:rows_piece])
        for y in range(count):
            value = code[y].astype(jnp.float32) * scale[offset + y : offset + y + 1]
            for h, part in enumerate(halves(value)):
                planes[h, pl.ds(base + y, core, stride=plane_rows), :] = part
        for h in range(cols // LANES):
            copy = pltpu.make_async_copy(
                planes.at[h].reshape(core, plane_rows, LANES).at[:, pl.ds(base, count)],
                out.at[:, pl.ds(base, count), pl.ds(h * LANES, LANES)],
                sem.at[index, h],
            )
            copy.start()
            copies.append(copy)
    for copy in copies:
        copy.wait()


def gather(view_id, pieces, codes, rows, views, tile=None):
    core, cols = codes[0].shape[1:]
    given = [] if tile is None else [tile]
    return pl.pallas_call(
        functools.partial(gather_kernel, pieces, rows // views, core, rows, cols),
        out_shape=jax.ShapeDtypeStruct((core, rows, cols), jnp.float32),
        in_specs=[SMEM] + [VMEM] * len(codes) + [ANY] * len(given),
        out_specs=ANY,
        scratch_shapes=[
            pltpu.VMEM((cols // LANES, core * (rows + PAD), LANES), jnp.float32),
            pltpu.SemaphoreType.DMA((len(codes), cols // LANES)),
        ],
        input_output_aliases={} if tile is None else {1 + len(codes): 0},
        compiler_params=pltpu.CompilerParams(vmem_limit_bytes=VMEM_LIMIT),
        name="gather",
    )(view_id, *codes, *given)


def band(taps, row_index, col_index):
    count = taps.shape[0]
    offsets = col_index[None, :] - row_index[:, None] + (count - 1) // 2
    chosen = offsets[None, :, :] == jnp.arange(count, dtype=jnp.int32)[:, None, None]
    return jnp.sum(jnp.where(chosen, taps[:, None, None], jnp.float32(0.0)), axis=0)


def on_device(estimate, views_data, psf_bank, psf_index, margin_extent):
    core, rows, cols = estimate.shape
    kernels_count = psf_bank.shape[0]
    tiles = lax.axis_size("tile")
    views = lax.axis_size("view")
    tile_id = lax.axis_index("tile")
    view_id = lax.axis_index("view")
    rows_piece = rows // views
    half = jnp.bfloat16

    near_pairs = [(t, t ^ 1) for t in range(tiles)]
    far_pairs = [(t, ((t + 1) ^ 1) - 1) for t in range(1, tiles - 1)]
    even = tile_id % 2 == 0

    def far(x):
        return lax.ppermute(x, "tile", far_pairs)

    def near(x):
        return lax.ppermute(x, "tile", near_pairs)

    def from_view(x, bits):
        return lax.ppermute(x, "view", [(v, v ^ bits) for v in range(views)])

    part = rows_piece // 2
    if views == 4:
        pieces = ((0, 0, rows_piece), (1, 0, rows_piece), (2, 0, rows_piece), (3, 0, part), (3, part, part))
    else:
        pieces = tuple((bits, 0, rows_piece) for bits in range(views))

    def share(x, send=None):
        send = send or (lambda y: y)
        sent = [send(x)]
        if views != 4:
            every = [x] + [from_view(x, bits) for bits in range(1, views)]
            return every, sent + [send(y) for y in every[1:]]
        one, two = from_view(x, 1), from_view(x, 2)
        sent += [send(one), send(two)]
        first, second = one[:part], two[part:]
        if x.shape[0] > rows_piece:
            first = jnp.concatenate([first, one[rows_piece:]], axis=0)
        rest = [from_view(first, 2), from_view(second, 1)]
        return [x, one, two, *rest], sent + [send(jnp.concatenate(rest, axis=0))]

    def own_rows(volume):
        return lax.dynamic_slice_in_dim(volume, view_id * rows_piece, rows_piece, axis=1)

    first_piece = jnp.transpose(own_rows(estimate).astype(half), (1, 0, 2))
    first_piece, volume, data = lax.optimization_barrier((first_piece, estimate, views_data[0]))
    far_piece = far(first_piece)
    bottom, top = data[:REACH], data[core - REACH :]
    to_far, to_near = jnp.where(even, bottom, top), jnp.where(even, top, bottom)
    far_piece, to_far, psf_bank, psf_index, margin_extent = lax.optimization_barrier(
        (far_piece, to_far, psf_bank, psf_index, margin_extent)
    )
    far_blocks, _ = share(far_piece)
    measured = (far(to_far), data, near(to_near))
    start = jnp.transpose(volume.astype(half), (1, 0, 2))
    blocks = [far_blocks, [start], [near(start)]]

    chosen = (jnp.arange(kernels_count, dtype=jnp.int32) == psf_index[0]).astype(jnp.float32)
    taps = jnp.einsum("k,kat->at", chosen, psf_bank.astype(jnp.float32))
    cores = jnp.arange(core, dtype=jnp.int32) + MARGIN
    below, above = jnp.where(even, 0, MARGIN + core), jnp.where(even, MARGIN + core, 0)
    deep = jnp.arange(MARGIN, dtype=jnp.int32)
    position = jnp.concatenate([deep + below, cores, deep + above])
    low_reach, high_reach = MARGIN - REACH, MARGIN + core
    thin = jnp.arange(REACH, dtype=jnp.int32)
    wanted = jnp.concatenate(
        [
            thin + jnp.where(even, low_reach, high_reach),
            cores,
            thin + jnp.where(even, high_reach, low_reach),
        ]
    )

    def inside(k):
        global_pos = tile_id * core - MARGIN + k
        held = (k >= MARGIN - margin_extent[0, 0]) & (k < MARGIN + core + margin_extent[0, 1])
        return held & (global_pos >= 0) & (global_pos < core * tiles)

    natural = jnp.arange(rows, dtype=jnp.int32)
    held = ((natural // rows_piece) ^ view_id) * rows_piece + natural % rows_piece
    columns = jnp.arange(cols, dtype=jnp.int32)
    z_band = jnp.where(inside(position)[None, :], band(taps[0], wanted, position), 0.0).astype(half)
    z_back = band(taps[0], wanted, cores).T.astype(half)
    y_band = band(taps[1], natural, held).astype(half)
    y_back = y_band.T
    x_back = band(taps[2], columns, columns).astype(half)
    x_band = x_back.T
    mask = inside(wanted).astype(jnp.int32)

    here = view_id.astype(jnp.int32).reshape(1)
    bands = (z_band, z_back, y_band, y_back, x_band, x_back)
    for it in range(ITERS):
        codes = list(sweep(here, mask, pieces, blocks, measured, bands, views))
        if it == 0:
            volume, codes[0] = lax.optimization_barrier((estimate, codes[0]))
            mine = jnp.transpose(own_rows(volume), (1, 0, 2))
        arrived = [codes[0]] + [from_view(codes[bits], bits) for bits in range(1, views)]
        if it + 1 < ITERS:
            mine, rounded = update(arrived, mine, False)
            own, fars = share(rounded, far)
            blocks = [fars, own, [near(x) for x in lax.optimization_barrier(tuple(own))]]
        else:
            (code,) = update(arrived, mine, True)
    codes, _ = share(code)
    early = min(3, len(codes))
    tile = gather(here, pieces[:early], codes[:early], rows, views)
    if early == len(codes):
        return tile
    return gather(here, pieces[early:], codes[early:], rows, views, tile)


def solution(mesh):
    return jax.shard_map(
        on_device,
        mesh=mesh,
        in_specs=(
            P("tile", None, None),
            P("view", "tile", None, None),
            P(),
            P("view"),
            P("tile", None),
        ),
        out_specs=P("tile", None, None),
        check_vma=False,
    )
```
